32 devices in a mesh: seg: 4 (over y, core), sec: 8 (over z, x).
Axes of the slice: x: 2, y: 2, z: 4, core: 2. Of those that a mesh axis runs over, the one named last changes fastest.
Arguments:
- wavefunction: bfloat16 [4, 8, 256, 256], P('seg'), may hold values from -6 to 6
- left_env: bfloat16 [4, 32, 8, 256, 256], P('seg', 'sec'), may hold values from -0.375 to 0.375
- right_env: bfloat16 [4, 32, 8, 256, 256], P('seg', 'sec'), may hold values from -0.375 to 0.375
- block_sizes: int32 [4, 8], P('seg'), may hold values from 64 to 256, as said below
Outputs:
- new_wavefunction: bfloat16 [4, 8, 256, 256], P('seg')
- incoming_left_env: bfloat16 [4, 32, 8, 256, 256], P('seg', 'sec')
- incoming_right_env: bfloat16 [4, 32, 8, 256, 256], P('seg', 'sec')
The draws below stay inside these ranges and needn't reach their ends.
Inputs may be any that keep to these rules, and one draw needn't show every extreme that they name: `block_sizes`: every block size is a multiple of 64; some block has size 256.
All inputs are finite; a program needn't handle non-finite values.
Results may differ from the reference program's by a relative error of at most 0.035.
Values may be sent and summed in bfloat16 or wider, within the bound.
No kernel may reach another device: no remote copies, remote signals or barrier semaphores. Data moves between devices by JAX's collectives and lax.ppermute only.
A program may use at most 64 MiB of HBM per device.

```python
import jax
import jax.numpy as jnp
from jax import lax

BLK = 256
QB = 64
KB = 8
W = 32
ITERS = 4
W_DEV = 4
SEGS = 4
N_SEC = 8


def draw_block_sizes(key, part):
    values = jax.random.randint(key, (SEGS, KB), 1, BLK // QB + 1) * QB
    return values.at[0, 0].set(BLK).astype(jnp.int32)


def block_levels(key, shape, split, least, largest):
    def one(axis_at, shards_of):
        steps = jax.random.uniform(jax.random.fold_in(jax.random.fold_in(key, 6), axis_at), (shards_of,), jnp.float32, least / len(split), largest / len(split))
        return jnp.repeat(jnp.exp(steps), shape[axis_at] // shards_of).reshape((-1,) + (1,) * (len(shape) - axis_at - 1))

    factor_of = one(*split[0])
    for cut in split[1:]:
        factor_of = factor_of * one(*cut)
    return factor_of


def bell_draw(own_key, shape, width, reach, shards=(), kind=jnp.bfloat16):
    drawn = jax.random.normal(own_key, shape, jnp.float32) * width
    if len(shards) > 0:
        drawn = block_levels(own_key, shape, shards, -0.22, 0.18) * drawn
    return jnp.clip(drawn, min=-reach, max=reach).astype(kind)


def setup_inputs(seed: int = 0) -> dict:
    keys = jax.random.split(jax.random.key(seed), 5)
    wavefunction = bell_draw(keys[0], (SEGS, KB, BLK, BLK), 1.0, 6.0, ((0, 4),))
    left_env = bell_draw(keys[1], (SEGS, W, KB, BLK, BLK), BLK ** -0.5, 0.375, ((0, 4), (1, 8)))
    right_env = bell_draw(keys[2], (SEGS, W, KB, BLK, BLK), BLK ** -0.5, 0.375, ((0, 4), (1, 8)))
    block_sizes = draw_block_sizes(jax.random.fold_in(keys[4], 71), 0)
    return dict(wavefunction=wavefunction, left_env=left_env, right_env=right_env, block_sizes=block_sizes)


epsilon = 1e-06

def settle(value):
    return lax.optimization_barrier(value.astype(jnp.bfloat16)).astype(jnp.float32)

def one_segment(inputs):
    wave, left, right, sizes = inputs
    index = jnp.arange(BLK)
    live = (index[None, :] < sizes[:, None]).astype(jnp.float32)
    mask = live[:, :, None] * live[:, None, :]
    start = wave.astype(jnp.float32) * mask
    state_tensor = (start / jnp.sqrt(jnp.mean(start * start) + epsilon)).astype(jnp.bfloat16)
    left_f = left.astype(jnp.float32)
    right_f = right.astype(jnp.float32)
    for iteration in range(ITERS):
        state_f = state_tensor.astype(jnp.float32)
        product = settle(jnp.einsum('wkab,kbc->wkac', left_f, state_f))
        terms = jnp.einsum('wkac,wkcd->wkad', product, right_f)
        grouped = terms.reshape(N_SEC, W_DEV, KB, BLK, BLK).sum(axis=1)
        applied = lax.optimization_barrier(jnp.sum(settle(grouped), axis=0)) / jnp.sqrt(jnp.float32(W))
        theta = jnp.sum(state_f * applied) / jnp.sum(state_f * state_f)
        update = mask * (state_f - (applied - theta * state_f))
        state_tensor = (update / jnp.sqrt(jnp.mean(update * update) + epsilon)).astype(jnp.bfloat16)
    state_f = state_tensor.astype(jnp.float32)
    scale_factor = jnp.sqrt(jnp.float32(BLK))
    left_portion = settle(jnp.einsum('kac,wkab->wkcb', state_f, left_f))
    built_left = (jnp.einsum('wkcb,kbd->wkcd', left_portion, state_f) / scale_factor).astype(jnp.bfloat16)
    right_portion = settle(jnp.einsum('kac,wkcd->wkad', state_f, right_f))
    built_right = (jnp.einsum('wkad,kbd->wkab', right_portion, state_f) / scale_factor).astype(jnp.bfloat16)
    return (state_tensor, built_left, built_right)

def reference(wavefunction, left_env, right_env, block_sizes):
    states, built_left, built_right = lax.map(one_segment, (wavefunction, left_env, right_env, block_sizes))
    blank = jnp.zeros_like(built_left[:1])
    incoming_left_env = jnp.concatenate([blank, built_left[:-1]], axis=0)
    incoming_right_env = jnp.concatenate([built_right[1:], blank], axis=0)
    return (states, incoming_left_env, incoming_right_env)
```

```python
import functools

import jax
import jax.numpy as jnp
from jax import lax
from jax.experimental import pallas as pl
from jax.experimental.pallas import tpu as pltpu
from jax.sharding import PartitionSpec as P

ITERS = 4
CHUNKS = 2
EPSILON = 1e-06


f32 = jnp.float32
bf16 = jnp.bfloat16
VMEM = pl.BlockSpec(memory_space=pltpu.VMEM)
SMEM = pl.BlockSpec(memory_space=pltpu.SMEM)
ANY = pl.BlockSpec(memory_space=pl.ANY)


def live_mask(size, blk):
    rows = lax.broadcasted_iota(jnp.int32, (blk, blk), 0)
    cols = lax.broadcasted_iota(jnp.int32, (blk, blk), 1)
    return (rows < size) & (cols < size)


def column_sums(value):
    rows, cols = value.shape
    return value.reshape(rows // 8, 8, cols).sum(axis=0)


def total(ref):
    acc = ref[0]
    for k in range(1, ref.shape[0]):
        acc = acc + ref[k]
    return jnp.sum(jnp.sum(acc, axis=0, keepdims=True), axis=1, keepdims=True)


def rayleigh(sector, pieces, u_ref, ss_ref, sa_ref):
    for p, piece in enumerate(pieces):
        k = sector[p]
        u = u_ref[k].astype(f32)
        ss_ref[k] = column_sums(u * u)
        sa_ref[k] = column_sums(u * piece[...].astype(f32))
    return total(ss_ref), total(sa_ref)


def step_scalars(ss, sa, count, root_channels):
    inverse = 1.0 / root_channels
    theta = sa * inverse / ss
    norm = 1.0 / jnp.sqrt(ss / count + EPSILON)
    return theta, norm, inverse


def fetch(l_hbm, r_hbm, lbuf, rbuf, sem, sector, base, groups):
    copies = []
    for m in range(groups):
        k = sector[base + m]
        pair = (
            pltpu.make_async_copy(l_hbm.at[:, k], lbuf.at[m], sem.at[0, m]),
            pltpu.make_async_copy(r_hbm.at[:, k], rbuf.at[m], sem.at[1, m]),
        )
        for copy in pair:
            copy.start()
        copies.append(pair)
    return copies


def apply_share(copies, lbuf, rbuf, u_ref, sector, base, outs):
    for m, out in enumerate(outs):
        width, blk = lbuf.shape[1], lbuf.shape[2]
        u = u_ref[sector[base + m]]
        copies[m][0].wait()
        product = jnp.dot(
            lbuf[m].reshape(width * blk, blk), u, preferred_element_type=f32
        ).astype(bf16)
        copies[m][1].wait()
        acc = jnp.dot(product[:blk], rbuf[m, 0], preferred_element_type=f32)
        for w in range(1, width):
            acc = acc + jnp.dot(
                product[w * blk : (w + 1) * blk], rbuf[m, w], preferred_element_type=f32
            )
        out[...] = acc.astype(bf16)


def first_kernel(groups, sector, sizes, wave, l_hbm, r_hbm, *rest):
    u_new, outs, (lbuf, rbuf, sem) = rest[0], rest[1 : 1 + groups], rest[1 + groups :]
    copies = fetch(l_hbm, r_hbm, lbuf, rbuf, sem, sector, 0, groups)
    blk = wave.shape[-1]
    for k in range(wave.shape[0]):
        u_new[k] = jnp.where(live_mask(sizes[k], blk), wave[k].astype(f32), 0.0).astype(bf16)
    apply_share(copies, lbuf, rbuf, u_new, sector, 0, outs)


def step_kernel(groups, root_channels, sector, sizes, u_ref, l_hbm, r_hbm, *rest):
    sectors, blk = u_ref.shape[0], u_ref.shape[-1]
    pieces, rest = rest[:sectors], rest[sectors:]
    u_new, outs, (lbuf, rbuf, sem, ss_ref, sa_ref) = (
        rest[0],
        rest[1 : 1 + groups],
        rest[1 + groups :],
    )
    copies = fetch(l_hbm, r_hbm, lbuf, rbuf, sem, sector, 0, groups)
    ss, sa = rayleigh(sector, pieces, u_ref, ss_ref, sa_ref)
    theta, norm, inverse = step_scalars(ss, sa, sectors * blk * blk, root_channels)
    keep = norm * (1.0 + theta)
    take = norm * inverse
    for p, piece in enumerate(pieces):
        k = sector[p]
        gone = jnp.where(live_mask(sizes[k], blk), piece[...].astype(f32), 0.0)
        u_new[k] = (keep * u_ref[k].astype(f32) - take * gone).astype(bf16)
    apply_share(copies, lbuf, rbuf, u_new, sector, 0, outs)


def share_kernel(groups, base, sector, u_ref, l_hbm, r_hbm, *rest):
    outs, (lbuf, rbuf, sem) = rest[:groups], rest[groups:]
    copies = fetch(l_hbm, r_hbm, lbuf, rbuf, sem, sector, base, groups)
    apply_share(copies, lbuf, rbuf, u_ref, sector, base, outs)


def last_kernel(root_channels, sector, sizes, u_ref, *rest):
    sectors, blk = u_ref.shape[0], u_ref.shape[-1]
    pieces, (state, full, ss_ref, sa_ref) = rest[:sectors], rest[sectors:]
    ss, sa = rayleigh(sector, pieces, u_ref, ss_ref, sa_ref)
    theta, norm, inverse = step_scalars(ss, sa, sectors * blk * blk, root_channels)
    keep = norm * (1.0 + theta)
    take = norm * inverse
    for p, piece in enumerate(pieces):
        k = sector[p]
        gone = jnp.where(live_mask(sizes[k], blk), piece[...].astype(f32), 0.0)
        update = keep * u_ref[k].astype(f32) - take * gone
        full[k] = update
        ss_ref[k] = column_sums(update * update)
    norm = 1.0 / jnp.sqrt(total(ss_ref) / (sectors * blk * blk) + EPSILON)
    for k in range(sectors):
        state[k] = (full[k] * norm).astype(bf16)


def build_kernel(state_l, state_r, l_ref, r_ref, out_l, out_r):
    width, blk = l_ref.shape[0], l_ref.shape[-1]
    scale = 1.0 / (float(blk) ** 0.5)
    s = state_l[0]
    for w in range(width):
        half = lax.dot_general(
            s, l_ref[w, 0], (((0,), (0,)), ((), ())), preferred_element_type=f32
        ).astype(bf16)
        out_l[w, 0] = (jnp.dot(half, s, preferred_element_type=f32) * scale).astype(bf16)
    t = state_r[0]
    for w in range(width):
        half = jnp.dot(t, r_ref[w, 0], preferred_element_type=f32).astype(bf16)
        out_r[w, 0] = (
            lax.dot_general(half, t, (((1,), (1,)), ((), ())), preferred_element_type=f32) * scale
        ).astype(bf16)


def passed_along(block, axis, distance):
    devices = range(lax.axis_size(axis))
    route = [(i - distance, i) for i in devices if i - distance in devices]
    return lax.ppermute(block, axis, route)


def swapped(block, bit):
    return lax.ppermute(block, "sec", [(i, i ^ bit) for i in range(lax.axis_size("sec"))])


def sum_over_sec(shares):
    groups = len(shares)
    got = [swapped(shares[m], m) for m in range(1, groups)]
    acc = shares[0].astype(f32)
    for other in got:
        acc = acc + other.astype(f32)
    acc = acc.astype(bf16)
    bit = groups
    while bit < lax.axis_size("sec"):
        acc = (acc.astype(f32) + swapped(acc, bit).astype(f32)).astype(bf16)
        bit *= 2
    return [acc] + [swapped(acc, m) for m in range(1, groups)]


def body(wavefunction, left_env, right_env, block_sizes):
    wave, left, right, sizes = wavefunction[0], left_env[0], right_env[0], block_sizes[0]
    width, sectors, blk = left.shape[0], left.shape[1], left.shape[-1]
    devices = lax.axis_size("sec")
    groups = sectors // CHUNKS
    assert groups & (groups - 1) == 0 and devices % groups == 0
    assert devices & (devices - 1) == 0
    root_channels = float(width * devices) ** 0.5

    left_before = passed_along(left, "seg", 1)
    right_after = passed_along(right, "seg", -1)

    me = lax.rem(lax.axis_index("sec"), groups)
    order = jnp.bitwise_xor(jnp.arange(groups, dtype=jnp.int32), me.astype(jnp.int32))
    sector = jnp.concatenate([order + h * groups for h in range(CHUNKS)])

    share = jax.ShapeDtypeStruct((blk, blk), bf16)
    whole = jax.ShapeDtypeStruct((sectors, blk, blk), bf16)
    env_scratch = [
        pltpu.VMEM((groups, width, blk, blk), bf16),
        pltpu.VMEM((groups, width, blk, blk), bf16),
        pltpu.SemaphoreType.DMA((2, groups)),
    ]
    sums = [pltpu.VMEM((sectors, 8, blk), f32)] * 2

    def call(kernel, in_specs, n_out, outs, scratch, name):
        return pl.pallas_call(
            kernel,
            in_specs=in_specs,
            out_specs=[VMEM] * n_out,
            out_shape=outs,
            scratch_shapes=scratch,
            name=name,
        )

    first = call(
        functools.partial(first_kernel, groups),
        [SMEM, SMEM, VMEM, ANY, ANY],
        1 + groups,
        [whole] + [share] * groups,
        env_scratch,
        "first",
    )
    step = call(
        functools.partial(step_kernel, groups, root_channels),
        [SMEM, SMEM, VMEM, ANY, ANY] + [VMEM] * sectors,
        1 + groups,
        [whole] + [share] * groups,
        env_scratch + sums,
        "step",
    )
    others = [
        call(
            functools.partial(share_kernel, groups, h * groups),
            [SMEM, VMEM, ANY, ANY],
            groups,
            [share] * groups,
            env_scratch,
            "share",
        )
        for h in range(1, CHUNKS)
    ]
    last = call(
        functools.partial(last_kernel, root_channels),
        [SMEM, SMEM, VMEM] + [VMEM] * sectors,
        1,
        [whole],
        [pltpu.VMEM((sectors, blk, blk), f32)] + sums,
        "last",
    )

    u, *shares = first(sector, sizes, wave, left, right)
    for iteration in range(ITERS):
        pieces = sum_over_sec(shares)
        for other in others:
            pieces += sum_over_sec(other(sector, u, left, right))
        if iteration < ITERS - 1:
            u, *shares = step(sector, sizes, u, left, right, *pieces)
    (state,) = last(sector, sizes, u, *pieces)

    state_before = passed_along(state, "seg", 1)
    state_after = passed_along(state, "seg", -1)
    one = pl.BlockSpec((1, blk, blk), lambda k: (k, 0, 0))
    env = pl.BlockSpec((width, 1, blk, blk), lambda k: (0, k, 0, 0))
    like = jax.ShapeDtypeStruct(left.shape, bf16)
    incoming_left, incoming_right = pl.pallas_call(
        build_kernel,
        grid=(sectors,),
        in_specs=[one, one, env, env],
        out_specs=[env, env],
        out_shape=[like, like],
        name="build",
    )(state_before, state_after, left_before, right_after)
    return (state[None], incoming_left[None], incoming_right[None])


def solution(mesh):
    env = P("seg", "sec", None, None, None)
    wave = P("seg", None, None, None)
    return jax.shard_map(
        body,
        mesh=mesh,
        in_specs=(wave, env, env, P("seg", None)),
        out_specs=(wave, env, env),
        check_vma=False,
    )
```

```python
import functools

import jax
import jax.numpy as jnp
from jax import lax
from jax.experimental import pallas as pl
from jax.experimental.pallas import tpu as pltpu
from jax.sharding import PartitionSpec as P

ITERS = 4
CHUNKS = 2
EPSILON = 1e-06
SCOPED = 12 * 2**20


f32 = jnp.float32
bf16 = jnp.bfloat16
VMEM = pl.BlockSpec(memory_space=pltpu.VMEM)
SMEM = pl.BlockSpec(memory_space=pltpu.SMEM)
HBM = pl.BlockSpec(memory_space=pltpu.HBM)


def live_mask(size, blk):
    rows = lax.broadcasted_iota(jnp.int32, (blk, blk), 0)
    cols = lax.broadcasted_iota(jnp.int32, (blk, blk), 1)
    return (rows < size) & (cols < size)


def column_sums(value):
    rows, cols = value.shape
    return value.reshape(rows // 8, 8, cols).sum(axis=0)


def total(ref):
    acc = ref[0]
    for k in range(1, ref.shape[0]):
        acc = acc + ref[k]
    return jnp.sum(jnp.sum(acc, axis=0, keepdims=True), axis=1, keepdims=True)


def sector_of(groups, p):
    me = lax.rem(lax.axis_index("sec"), groups)
    return lax.bitwise_xor(me, p % groups) + (p // groups) * groups


def rayleigh(groups, pieces, u_ref, ss_ref, sa_ref):
    for p, piece in enumerate(pieces):
        k = sector_of(groups, p)
        u = u_ref[k].astype(f32)
        ss_ref[k] = column_sums(u * u)
        sa_ref[k] = column_sums(u * piece[...].astype(f32))
    return total(ss_ref), total(sa_ref)


def step_scalars(ss, sa, count, root_channels):
    inverse = 1.0 / root_channels
    theta = sa * inverse / ss
    norm = 1.0 / jnp.sqrt(ss / count + EPSILON)
    return norm * (1.0 + theta), norm * inverse


def multiply_left(l_ref, k, u_ref, out):
    width, blk = l_ref.shape[1], l_ref.shape[2]
    out[...] = jnp.dot(
        l_ref[k].reshape(width * blk, blk), u_ref[k], preferred_element_type=f32
    ).astype(bf16)


def multiply_right(product, r_ref, k, out):
    width, blk = r_ref.shape[1], r_ref.shape[2]
    acc = jnp.dot(product[:blk, :], r_ref[k, 0], preferred_element_type=f32)
    for w in range(1, width):
        rows = product[w * blk : (w + 1) * blk, :]
        acc = acc + jnp.dot(rows, r_ref[k, w], preferred_element_type=f32)
    out[...] = acc.astype(bf16)


def apply_share(groups, base, l_ref, r_ref, u_ref, product, outs, ready=None):
    ks = [sector_of(groups, base + m) for m in range(groups)]

    def begin(m):
        if ready is not None:
            ready(m)
        multiply_left(l_ref, ks[m], u_ref, product.at[m % 2])

    begin(0)
    for m in range(groups):
        if m + 1 < groups:
            begin(m + 1)
        multiply_right(product.at[m % 2], r_ref, ks[m], outs[m])


def first_kernel(groups, sizes, wave, l_hbm, r_hbm, *rest):
    u_new, l_ref, r_ref = rest[:3]
    outs, (start, product, sem) = rest[3 : 3 + groups], rest[3 + groups :]
    sectors, blk = start.shape[0], start.shape[-1]
    copies = []
    for p in range(sectors):
        k = sector_of(groups, p)
        three = (
            pltpu.make_async_copy(wave.at[k], start.at[k], sem.at[0, p]),
            pltpu.make_async_copy(l_hbm.at[:, k], l_ref.at[k], sem.at[1, p]),
            pltpu.make_async_copy(r_hbm.at[:, k], r_ref.at[k], sem.at[2, p]),
        )
        for copy in three:
            copy.start()
        copies.append(three)

    def ready(p):
        for copy in copies[p]:
            copy.wait()
        k = sector_of(groups, p)
        u_new[k] = jnp.where(live_mask(sizes[0, k], blk), start[k].astype(f32), 0.0).astype(bf16)

    apply_share(groups, 0, l_ref, r_ref, u_new, product, outs, ready)
    for p in range(groups, sectors):
        ready(p)


def step_kernel(groups, root_channels, sizes, u_ref, l_ref, r_ref, *rest):
    sectors, blk = u_ref.shape[0], u_ref.shape[-1]
    pieces, rest = rest[:sectors], rest[sectors:]
    u_new, outs, (product, ss_ref, sa_ref) = rest[0], rest[1 : 1 + groups], rest[1 + groups :]
    ss, sa = rayleigh(groups, pieces, u_ref, ss_ref, sa_ref)
    keep, take = step_scalars(ss, sa, sectors * blk * blk, root_channels)

    def ready(p):
        k = sector_of(groups, p)
        gone = jnp.where(live_mask(sizes[0, k], blk), pieces[p][...].astype(f32), 0.0)
        u_new[k] = (keep * u_ref[k].astype(f32) - take * gone).astype(bf16)

    apply_share(groups, 0, l_ref, r_ref, u_new, product, outs, ready)
    for p in range(groups, sectors):
        ready(p)


def share_kernel(groups, base, u_ref, l_ref, r_ref, *rest):
    outs, (product,) = rest[:groups], rest[groups:]
    apply_share(groups, base, l_ref, r_ref, u_ref, product, outs)


def last_kernel(groups, root_channels, sizes, u_ref, *rest):
    sectors, blk = u_ref.shape[0], u_ref.shape[-1]
    pieces, (state, full, ss_ref, sa_ref) = rest[:sectors], rest[sectors:]
    ss, sa = rayleigh(groups, pieces, u_ref, ss_ref, sa_ref)
    keep, take = step_scalars(ss, sa, sectors * blk * blk, root_channels)
    for p, piece in enumerate(pieces):
        k = sector_of(groups, p)
        gone = jnp.where(live_mask(sizes[0, k], blk), piece[...].astype(f32), 0.0)
        update = keep * u_ref[k].astype(f32) - take * gone
        full[k] = update
        ss_ref[k] = column_sums(update * update)
    norm = 1.0 / jnp.sqrt(total(ss_ref) / (sectors * blk * blk) + EPSILON)
    for k in range(sectors):
        state[k] = (full[k] * norm).astype(bf16)


def build_kernel(state_l, state_r, l_ref, r_ref, out_l, out_r):
    width, blk = l_ref.shape[0], l_ref.shape[-1]
    scale = 1.0 / (float(blk) ** 0.5)
    s = state_l[0]
    for w in range(width):
        half = lax.dot_general(
            s, l_ref[w, 0], (((0,), (0,)), ((), ())), preferred_element_type=f32
        ).astype(bf16)
        out_l[w, 0] = (jnp.dot(half, s, preferred_element_type=f32) * scale).astype(bf16)
    t = state_r[0]
    for w in range(width):
        half = jnp.dot(t, r_ref[w, 0], preferred_element_type=f32).astype(bf16)
        out_r[w, 0] = (
            lax.dot_general(half, t, (((1,), (1,)), ((), ())), preferred_element_type=f32) * scale
        ).astype(bf16)


def passed_along(block, axis, distance):
    devices = range(lax.axis_size(axis))
    route = [(i - distance, i) for i in devices if i - distance in devices]
    return lax.ppermute(block, axis, route)


def swapped(block, bit):
    return lax.ppermute(block, "sec", [(i, i ^ bit) for i in range(lax.axis_size("sec"))])


def sum_over_sec(shares):
    groups = len(shares)
    got = [swapped(shares[m], m) for m in range(1, groups)]
    acc = shares[0].astype(f32)
    for other in got:
        acc = acc + other.astype(f32)
    acc = acc.astype(bf16)
    bit = groups
    while bit < lax.axis_size("sec"):
        acc = (acc.astype(f32) + swapped(acc, bit).astype(f32)).astype(bf16)
        bit *= 2
    return [acc] + [swapped(acc, m) for m in range(1, groups)]


def body(wavefunction, left_env, right_env, block_sizes):
    wave, left, right = wavefunction[0], left_env[0], right_env[0]
    width, sectors, blk = left.shape[0], left.shape[1], left.shape[-1]
    devices = lax.axis_size("sec")
    groups = sectors // CHUNKS
    assert groups & (groups - 1) == 0 and devices % groups == 0
    assert devices & (devices - 1) == 0
    root_channels = float(width * devices) ** 0.5

    left_before = passed_along(left, "seg", 1)
    right_after = passed_along(right, "seg", -1)

    share = pltpu.VMEM((blk, blk), bf16)
    whole = pltpu.VMEM((sectors, blk, blk), bf16)
    env = pltpu.VMEM((sectors, width, blk, blk), bf16)
    product = pltpu.VMEM((2, width * blk, blk), bf16)
    sums = [pltpu.VMEM((sectors, 8, blk), f32)] * 2

    def call(kernel, in_specs, outs, scratch, name):
        run = pl.pallas_call(
            kernel,
            in_specs=in_specs,
            out_specs=[VMEM] * len(outs),
            out_shape=outs,
            scratch_shapes=scratch,
            compiler_params=pltpu.CompilerParams(vmem_limit_bytes=SCOPED),
            name=name,
        )

        def on_chip(*args):
            return run(
                *(
                    arg if spec is SMEM else pltpu.with_memory_space_constraint(arg, spec.memory_space)
                    for arg, spec in zip(args, in_specs)
                )
            )

        return on_chip

    first = call(
        functools.partial(first_kernel, groups),
        [SMEM, HBM, HBM, HBM],
        [whole, env, env] + [share] * groups,
        [whole, product, pltpu.SemaphoreType.DMA((3, sectors))],
        "first",
    )
    step = call(
        functools.partial(step_kernel, groups, root_channels),
        [SMEM, VMEM, VMEM, VMEM] + [VMEM] * sectors,
        [whole] + [share] * groups,
        [product] + sums,
        "step",
    )
    others = [
        call(
            functools.partial(share_kernel, groups, h * groups),
            [VMEM, VMEM, VMEM],
            [share] * groups,
            [product],
            "share",
        )
        for h in range(1, CHUNKS)
    ]
    last = call(
        functools.partial(last_kernel, groups, root_channels),
        [SMEM, VMEM] + [VMEM] * sectors,
        [whole],
        [pltpu.VMEM((sectors, blk, blk), f32)] + sums,
        "last",
    )

    u, l_held, r_held, *shares = first(block_sizes, wave, left, right)
    for iteration in range(ITERS):
        pieces = sum_over_sec(shares)
        for other in others:
            pieces += sum_over_sec(other(u, l_held, r_held))
        if iteration < ITERS - 1:
            u, *shares = step(block_sizes, u, l_held, r_held, *pieces)
    (state,) = last(block_sizes, u, *pieces)

    state_before = passed_along(state, "seg", 1)
    state_after = passed_along(state, "seg", -1)
    one = pl.BlockSpec((1, blk, blk), lambda k: (k, 0, 0))
    four = pl.BlockSpec((width, 1, blk, blk), lambda k: (0, k, 0, 0))
    like = jax.ShapeDtypeStruct(left.shape, bf16)
    incoming_left, incoming_right = pl.pallas_call(
        build_kernel,
        grid=(sectors,),
        in_specs=[one, one, four, four],
        out_specs=[four, four],
        out_shape=[like, like],
        compiler_params=pltpu.CompilerParams(vmem_limit_bytes=2 * SCOPED),
        name="build",
    )(state_before, state_after, left_before, right_after)
    return (state[None], incoming_left[None], incoming_right[None])


def solution(mesh):
    env = P("seg", "sec", None, None, None)
    wave = P("seg", None, None, None)
    return jax.shard_map(
        body,
        mesh=mesh,
        in_specs=(wave, env, env, P("seg", None)),
        out_specs=(wave, env, env),
        check_vma=False,
    )
```

```python
import functools

import jax
import jax.numpy as jnp
from jax import lax
from jax.experimental import pallas as pl
from jax.experimental.pallas import tpu as pltpu
from jax.sharding import PartitionSpec as P

ITERS = 4
CHUNKS = 2
EARLY = (3, 4)
EPSILON = 1e-06
SCOPED = 12 * 2**20


f32 = jnp.float32
bf16 = jnp.bfloat16
VMEM = pl.BlockSpec(memory_space=pltpu.VMEM)
SMEM = pl.BlockSpec(memory_space=pltpu.SMEM)
HBM = pl.BlockSpec(memory_space=pltpu.HBM)


def live_mask(size, blk):
    rows = lax.broadcasted_iota(jnp.int32, (blk, blk), 0)
    cols = lax.broadcasted_iota(jnp.int32, (blk, blk), 1)
    return (rows < size) & (cols < size)


def column_sums(value):
    rows, cols = value.shape
    return value.reshape(rows // 8, 8, cols).sum(axis=0)


def total(ref):
    acc = ref[0]
    for k in range(1, ref.shape[0]):
        acc = acc + ref[k]
    return jnp.sum(jnp.sum(acc, axis=0, keepdims=True), axis=1, keepdims=True)


def sector_of(groups, p):
    me = lax.rem(lax.axis_index("sec"), groups)
    return lax.bitwise_xor(me, p % groups) + (p // groups) * groups


def summed(groups, early, late, p):
    if p < groups:
        rows = early[p].shape[-1] - early[p].shape[0]
        return jnp.concatenate([early[p][...], late[p][:rows, :]], axis=0).astype(f32)
    m = p - groups
    return late[m][late[m].shape[0] - late[m].shape[1] :, :].astype(f32)


def rayleigh(groups, early, late, u_ref, ss_ref, sa_ref):
    for p in range(u_ref.shape[0]):
        k = sector_of(groups, p)
        u = u_ref[k].astype(f32)
        ss_ref[k] = column_sums(u * u)
        sa_ref[k] = column_sums(u * summed(groups, early, late, p))
    return total(ss_ref), total(sa_ref)


def step_scalars(ss, sa, count, root_channels):
    inverse = 1.0 / root_channels
    theta = sa * inverse / ss
    norm = 1.0 / jnp.sqrt(ss / count + EPSILON)
    return norm * (1.0 + theta), norm * inverse


def multiply_left(l_ref, k, u_ref, out):
    width, blk = l_ref.shape[1], l_ref.shape[2]
    out[...] = jnp.dot(
        l_ref[k].reshape(width * blk, blk), u_ref[k], preferred_element_type=f32
    ).astype(bf16)


def multiply_right(product, r_ref, k):
    width, blk = r_ref.shape[1], r_ref.shape[2]
    acc = jnp.dot(product[:blk, :], r_ref[k, 0], preferred_element_type=f32)
    for w in range(1, width):
        rows = product[w * blk : (w + 1) * blk, :]
        acc = acc + jnp.dot(rows, r_ref[k, w], preferred_element_type=f32)
    return acc.astype(bf16)


def apply_share(groups, base, l_ref, r_ref, u_ref, product, put, ready=None):
    ks = [sector_of(groups, base + m) for m in range(groups)]

    def begin(m):
        if ready is not None:
            ready(m)
        multiply_left(l_ref, ks[m], u_ref, product.at[m % 2])

    begin(0)
    for m in range(groups):
        if m + 1 < groups:
            begin(m + 1)
        put(m, multiply_right(product.at[m % 2], r_ref, ks[m]))


def put_early(early, rest):
    def put(m, value):
        rows = early[m].shape[0]
        early[m][...] = value[:rows, :]
        rest[m] = value[rows:, :]

    return put


def first_kernel(groups, sizes, wave, l_hbm, r_hbm, *rest):
    u_new, l_ref, r_ref, held = rest[:4]
    early, (start, product, sem) = rest[4 : 4 + groups], rest[4 + groups :]
    sectors, blk = start.shape[0], start.shape[-1]
    copies = []
    for p in range(sectors):
        k = sector_of(groups, p)
        three = (
            pltpu.make_async_copy(wave.at[k], start.at[k], sem.at[0, p]),
            pltpu.make_async_copy(l_hbm.at[:, k], l_ref.at[k], sem.at[1, p]),
            pltpu.make_async_copy(r_hbm.at[:, k], r_ref.at[k], sem.at[2, p]),
        )
        for copy in three:
            copy.start()
        copies.append(three)

    def ready(p):
        for copy in copies[p]:
            copy.wait()
        k = sector_of(groups, p)
        u_new[k] = jnp.where(live_mask(sizes[0, k], blk), start[k].astype(f32), 0.0).astype(bf16)

    apply_share(groups, 0, l_ref, r_ref, u_new, product, put_early(early, held), ready)
    for p in range(groups, sectors):
        ready(p)


def step_kernel(groups, root_channels, sizes, u_ref, l_ref, r_ref, *rest):
    sectors, blk = u_ref.shape[0], u_ref.shape[-1]
    summed_early, summed_late, rest = rest[:groups], rest[groups : 2 * groups], rest[2 * groups :]
    u_new, held = rest[:2]
    early, (product, ss_ref, sa_ref) = rest[2 : 2 + groups], rest[2 + groups :]
    ss, sa = rayleigh(groups, summed_early, summed_late, u_ref, ss_ref, sa_ref)
    keep, take = step_scalars(ss, sa, sectors * blk * blk, root_channels)

    def ready(p):
        k = sector_of(groups, p)
        gone = jnp.where(
            live_mask(sizes[0, k], blk), summed(groups, summed_early, summed_late, p), 0.0
        )
        u_new[k] = (keep * u_ref[k].astype(f32) - take * gone).astype(bf16)

    apply_share(groups, 0, l_ref, r_ref, u_new, product, put_early(early, held), ready)
    for p in range(groups, sectors):
        ready(p)


def share_kernel(groups, u_ref, l_ref, r_ref, held, *rest):
    late, (product,) = rest[:groups], rest[groups:]
    rows = held.shape[1]

    def put(m, value):
        late[m][:rows, :] = held[m]
        late[m][rows:, :] = value

    apply_share(groups, groups, l_ref, r_ref, u_ref, product, put)


def last_kernel(groups, root_channels, sizes, u_ref, *rest):
    sectors, blk = u_ref.shape[0], u_ref.shape[-1]
    early, late, rest = rest[:groups], rest[groups : 2 * groups], rest[2 * groups :]
    state, parts, (full, ss_ref, sa_ref) = rest[0], rest[1:-3], rest[-3:]
    ss, sa = rayleigh(groups, early, late, u_ref, ss_ref, sa_ref)
    keep, take = step_scalars(ss, sa, sectors * blk * blk, root_channels)
    for p in range(sectors):
        k = sector_of(groups, p)
        gone = jnp.where(live_mask(sizes[0, k], blk), summed(groups, early, late, p), 0.0)
        update = keep * u_ref[k].astype(f32) - take * gone
        full[k] = update
        ss_ref[k] = column_sums(update * update)
    norm = 1.0 / jnp.sqrt(total(ss_ref) / (sectors * blk * blk) + EPSILON)
    k = 0
    for part in parts:
        for i in range(part.shape[0]):
            value = (full[k] * norm).astype(bf16)
            state[k] = value
            part[i] = value
            k += 1


def build_kernel(state_l, state_r, l_ref, r_ref, *rest):
    out_l, out_r = rest[-2:]
    width, blk = l_ref.shape[0], l_ref.shape[-1]
    scale = 1.0 / (float(blk) ** 0.5)
    s = state_l[0]
    for w in range(width):
        half = lax.dot_general(
            s, l_ref[w, 0], (((0,), (0,)), ((), ())), preferred_element_type=f32
        ).astype(bf16)
        out_l[w, 0] = (jnp.dot(half, s, preferred_element_type=f32) * scale).astype(bf16)
    t = state_r[0]
    for w in range(width):
        half = jnp.dot(t, r_ref[w, 0], preferred_element_type=f32).astype(bf16)
        out_r[w, 0] = (
            lax.dot_general(half, t, (((1,), (1,)), ((), ())), preferred_element_type=f32) * scale
        ).astype(bf16)


def passed_along(block, axis, distance):
    devices = range(lax.axis_size(axis))
    route = [(i - distance, i) for i in devices if i - distance in devices]
    return lax.ppermute(block, axis, route)


def swapped(block, bit):
    return lax.ppermute(block, "sec", [(i, i ^ bit) for i in range(lax.axis_size("sec"))])


def sum_over_sec(shares):
    groups = len(shares)
    got = [swapped(shares[m], m) for m in range(1, groups)]
    acc = shares[0].astype(f32)
    for other in got:
        acc = acc + other.astype(f32)
    acc = acc.astype(bf16)
    bit = groups
    while bit < lax.axis_size("sec"):
        acc = (acc.astype(f32) + swapped(acc, bit).astype(f32)).astype(bf16)
        bit *= 2
    return [acc] + [swapped(acc, m) for m in range(1, groups)]


def body(wavefunction, left_env, right_env, block_sizes):
    wave, left, right = wavefunction[0], left_env[0], right_env[0]
    width, sectors, blk = left.shape[0], left.shape[1], left.shape[-1]
    devices = lax.axis_size("sec")
    groups = sectors // CHUNKS
    assert groups & (groups - 1) == 0 and devices % groups == 0
    assert devices & (devices - 1) == 0
    root_channels = float(width * devices) ** 0.5

    left_before = passed_along(left, "seg", 1)
    right_after = passed_along(right, "seg", -1)

    assert sectors == CHUNKS * groups
    first_rows = blk * EARLY[0] // EARLY[1]
    early = [pltpu.VMEM((first_rows, blk), bf16)] * groups
    held = pltpu.VMEM((groups, blk - first_rows, blk), bf16)
    late = [pltpu.VMEM((2 * blk - first_rows, blk), bf16)] * groups
    whole = pltpu.VMEM((sectors, blk, blk), bf16)
    env = pltpu.VMEM((sectors, width, blk, blk), bf16)
    product = pltpu.VMEM((2, width * blk, blk), bf16)
    sums = [pltpu.VMEM((sectors, 8, blk), f32)] * 2

    def call(kernel, in_specs, outs, scratch, name):
        run = pl.pallas_call(
            kernel,
            in_specs=in_specs,
            out_specs=[VMEM] * len(outs),
            out_shape=outs,
            scratch_shapes=scratch,
            compiler_params=pltpu.CompilerParams(vmem_limit_bytes=SCOPED),
            name=name,
        )

        def on_chip(*args):
            return run(
                *(
                    arg if spec is SMEM else pltpu.with_memory_space_constraint(arg, spec.memory_space)
                    for arg, spec in zip(args, in_specs)
                )
            )

        return on_chip

    first = call(
        functools.partial(first_kernel, groups),
        [SMEM, HBM, HBM, HBM],
        [whole, env, env, held] + early,
        [whole, product, pltpu.SemaphoreType.DMA((3, sectors))],
        "first",
    )
    step = call(
        functools.partial(step_kernel, groups, root_channels),
        [SMEM, VMEM, VMEM, VMEM] + [VMEM] * sectors,
        [whole, held] + early,
        [product] + sums,
        "step",
    )
    second = call(
        functools.partial(share_kernel, groups),
        [VMEM, VMEM, VMEM, VMEM],
        late,
        [product],
        "second",
    )
    counts = [sectors // 2, sectors // 4, sectors - sectors // 2 - sectors // 4]
    last = call(
        functools.partial(last_kernel, groups, root_channels),
        [SMEM, VMEM] + [VMEM] * sectors,
        [whole] + [pltpu.VMEM((count, blk, blk), bf16) for count in counts],
        [pltpu.VMEM((sectors, blk, blk), f32)] + sums,
        "last",
    )

    u, l_held, r_held, rest, *shares = first(block_sizes, wave, left, right)
    for iteration in range(ITERS):
        pieces = sum_over_sec(shares)
        pieces += sum_over_sec(second(u, l_held, r_held, rest))
        if iteration < ITERS - 1:
            u, rest, *shares = step(block_sizes, u, l_held, r_held, *pieces)
    state, *parts = last(block_sizes, u, *pieces)

    moved = [(passed_along(part, "seg", 1), passed_along(part, "seg", -1)) for part in parts]
    like = jax.ShapeDtypeStruct(left.shape, bf16)
    one = pl.BlockSpec((1, blk, blk), lambda k: (k, 0, 0))
    built, base = (), 0
    for count, (state_before, state_after) in zip(counts, moved):
        four = pl.BlockSpec((width, 1, blk, blk), lambda k, base=base: (0, base + k, 0, 0))
        built = pl.pallas_call(
            build_kernel,
            grid=(count,),
            in_specs=[one, one, four, four] + [pl.BlockSpec(memory_space=pl.ANY)] * len(built),
            out_specs=[four, four],
            out_shape=[like, like],
            input_output_aliases={4: 0, 5: 1} if built else {},
            compiler_params=pltpu.CompilerParams(vmem_limit_bytes=2 * SCOPED),
            name="build",
        )(state_before, state_after, left_before, right_after, *built)
        base += count
    incoming_left, incoming_right = built
    return (state[None], incoming_left[None], incoming_right[None])


def solution(mesh):
    env = P("seg", "sec", None, None, None)
    wave = P("seg", None, None, None)
    return jax.shard_map(
        body,
        mesh=mesh,
        in_specs=(wave, env, env, P("seg", None)),
        out_specs=(wave, env, env),
        check_vma=False,
    )
```
